512 devices in a mesh: dp: 32 (over z_lo, x), tensor: 16 (over z_hi, y, core).
Axes of the slice: x: 4, y: 4, z: 16 (z_hi: 2, z_lo: 8; z = z_hi * 8 + z_lo), core: 2. Of those that a mesh axis runs over, the one named last changes fastest.
Arguments:
- out_grad: bfloat16 [4096, 4096], P(('dp', 'tensor')), may hold values from -6 to 6
- gate_pre: bfloat16 [4096, 14336], P('dp', 'tensor'), may hold values from -6 to 6
- up_pre: bfloat16 [4096, 14336], P('dp', 'tensor'), may hold values from -6 to 6
- down_weight: bfloat16 [14336, 4096], P('tensor', 'dp'), may hold values from -6 to 6
- moment: float32 [14336, 4096], P('tensor', 'dp'), may hold values from -4 to 4
- second: float32 [14336, 4096], P('tensor', 'dp'), may hold values from 0.01 to 0.5
- decay_mask: int32 [14336], P('tensor'), may hold values 0 or 1
Outputs:
- grad_gate: bfloat16 [4096, 14336], P('dp', 'tensor')
- grad_up: bfloat16 [4096, 14336], P('dp', 'tensor')
- new_weight: bfloat16 [14336, 4096], P('tensor', 'dp')
- new_moment: float32 [14336, 4096], P('tensor', 'dp')
- new_second: float32 [14336, 4096], P('tensor', 'dp')
The draws below stay inside these ranges and needn't reach their ends.
All inputs are finite; a program needn't handle non-finite values. No bound on the sum of `decay_mask` on one device may be relied on, other than what follows from the above.
Results may differ from the reference program's by a relative error of at most 0.0014.
Values may be sent and summed in bfloat16 or wider, within the bound.
A program may use at most 64 MiB of HBM per device.

```python
import math
import jax
import jax.numpy as jnp

D = 4096
FF = 14336
OPT_STEP = 10
TOKENS = 4096


def touch_ends(array, own_key, least, top_value):
    shape = array.shape
    spot = [jax.random.randint(jax.random.fold_in(own_key, axis), (), 0, shape[axis]) for axis in range(len(shape))]
    array = array.at[tuple(spot)].set(least)
    longest = shape.index(max(shape))
    spot[longest] = (spot[longest] + 1) % shape[longest]
    return array.at[tuple(spot)].set(top_value)


def levels(key, shape, split, smallest, largest):
    def one(axis_at, shards_of):
        draws = jax.random.uniform(jax.random.fold_in(jax.random.fold_in(key, 6), axis_at), (shards_of,), jnp.float32, smallest / len(split), largest / len(split))
        return jnp.repeat(jnp.exp(draws), shape[axis_at] // shards_of).reshape((-1,) + (1,) * (len(shape) - axis_at - 1))

    gain = one(*split[0])
    for cut in split[1:]:
        gain = gain * one(*cut)
    return gain


def bell_draw(own_key, shape, spread, most, cuts=(), kind=jnp.bfloat16):
    drawn = jax.random.normal(own_key, shape, jnp.float32) * spread
    if len(cuts) > 0:
        drawn = levels(own_key, shape, cuts, -0.22, 0.18) * drawn
    return jnp.clip(drawn, min=-most, max=most).astype(kind)


def setup_inputs(seed: int = 0) -> dict:
    splits = jax.random.split(jax.random.key(seed), 8)
    out_grad = bell_draw(splits[0], (TOKENS, D), 1.0, 6.0, ((0, 512),))
    gate_pre = bell_draw(splits[1], (TOKENS, FF), 1.0, 6.0, ((0, 32), (1, 16)))
    up_pre = bell_draw(splits[2], (TOKENS, FF), 1.0, 6.0, ((0, 32), (1, 16)))
    down_weight = bell_draw(splits[3], (FF, D), 1.0, 6.0, ((0, 16), (1, 32)))
    moment = bell_draw(splits[4], (FF, D), 0.3, 4.0, ((0, 16), (1, 32)), jnp.float32)
    second = jnp.clip(jnp.exp(math.log(0.5) - 3.912023 * jax.random.uniform(splits[5], (FF, D), jnp.float32) ** levels(splits[5], (FF, D), ((0, 16), (1, 32)), -0.2, 0.2)), 0.01, 0.5)
    decay_mask = touch_ends((jax.random.randint(splits[6], (FF,), 0, 2) < 1).astype(jnp.int32), jax.random.fold_in(splits[6], 1), 0, 1)
    return {"out_grad": out_grad, "gate_pre": gate_pre, "up_pre": up_pre, "down_weight": down_weight, "moment": moment, "second": second, "decay_mask": decay_mask}


BETA_ONE = 0.9
BETA_TWO = 0.95
LEARN_RATE = 0.1
DECAY_RATE = 0.5
ADAM_EPS = 1e-08

def reference(out_grad, gate_pre, up_pre, down_weight, moment, second, decay_mask):
    factor = 1.0 / math.sqrt(FF)
    gate = gate_pre.astype(jnp.float32)
    up = up_pre.astype(jnp.float32)
    sigmoid_gate = jax.nn.sigmoid(gate)
    activated = gate * sigmoid_gate
    hidden = (activated * up).astype(jnp.bfloat16)
    back = jnp.dot(out_grad, down_weight.T, preferred_element_type=jnp.float32) * factor
    grad_up = (back * activated).astype(jnp.bfloat16)
    grad_gate = (back * up * sigmoid_gate * (1.0 + gate * (1.0 - sigmoid_gate))).astype(jnp.bfloat16)
    weight_grad = jnp.dot(hidden.T, out_grad, preferred_element_type=jnp.float32) * factor
    new_moment = BETA_ONE * moment + (1.0 - BETA_ONE) * weight_grad
    new_second = BETA_TWO * second + (1.0 - BETA_TWO) * weight_grad * weight_grad
    fix_one = 1.0 - BETA_ONE ** OPT_STEP
    fix_two = 1.0 - BETA_TWO ** OPT_STEP
    weight = down_weight.astype(jnp.float32)
    decay = decay_mask.astype(jnp.float32)[:, None]
    direction = new_moment / fix_one / (jnp.sqrt(new_second / fix_two) + ADAM_EPS) + DECAY_RATE * decay * weight
    new_weight = (weight - LEARN_RATE * direction).astype(jnp.bfloat16)
    return (grad_gate, grad_up, new_weight, new_moment, new_second)
```

```python
import math

import jax
import jax.numpy as jnp
from jax import lax
from jax.sharding import Mesh
from jax.sharding import PartitionSpec as P

FF = 14336
OPT_STEP = 10


BETA_ONE = 0.9
BETA_TWO = 0.95
LEARN_RATE = 0.1
DECAY_RATE = 0.5
ADAM_EPS = 1e-08

DP = ("zl", "x")
TP = ("zh", "y", "c")


def body(out_grad, gate_pre, up_pre, down_weight, moment, second, decay_mask):
    factor = 1.0 / math.sqrt(FF)
    group_grad = lax.all_gather(out_grad, "c", axis=0, tiled=True)
    group_grad = lax.all_gather(group_grad, "y", axis=0, tiled=True)
    group_grad = lax.all_gather(group_grad, "zh", axis=0, tiled=True)
    gate = gate_pre.astype(jnp.float32)
    up = up_pre.astype(jnp.float32)
    sigmoid_gate = jax.nn.sigmoid(gate)
    activated = gate * sigmoid_gate
    hidden = (activated * up).astype(jnp.bfloat16)
    columns = lax.all_to_all(group_grad, DP, split_axis=1, concat_axis=0, tiled=True)
    stacked = jnp.stack([down_weight, hidden.T])
    stacked = lax.all_gather(stacked, "x", axis=2, tiled=True)
    stacked = lax.all_gather(stacked, "zl", axis=2, tiled=True)
    back_sum = lax.dot_general(
        group_grad,
        stacked[0],
        (((1,), (1,)), ((), ())),
        preferred_element_type=jnp.float32,
    )
    grad_sum = lax.dot_general(
        stacked[1],
        columns,
        (((1,), (0,)), ((), ())),
        preferred_element_type=jnp.float32,
    )
    back = back_sum * factor
    grad_up = (back * activated).astype(jnp.bfloat16)
    grad_gate = (back * up * sigmoid_gate * (1.0 + gate * (1.0 - sigmoid_gate))).astype(
        jnp.bfloat16
    )
    weight_grad = grad_sum * factor
    new_moment = BETA_ONE * moment + (1.0 - BETA_ONE) * weight_grad
    new_second = BETA_TWO * second + (1.0 - BETA_TWO) * weight_grad * weight_grad
    fix_one = 1.0 - BETA_ONE**OPT_STEP
    fix_two = 1.0 - BETA_TWO**OPT_STEP
    weight = down_weight.astype(jnp.float32)
    decay = decay_mask.astype(jnp.float32)[:, None]
    direction = (
        new_moment / fix_one / (jnp.sqrt(new_second / fix_two) + ADAM_EPS)
        + DECAY_RATE * decay * weight
    )
    new_weight = (weight - LEARN_RATE * direction).astype(jnp.bfloat16)
    return (grad_gate, grad_up, new_weight, new_moment, new_second)


def solution(mesh):
    zl, x = 8, mesh.shape["dp"] // 8
    zh = mesh.shape["tensor"] // 8
    fine = Mesh(mesh.devices.reshape(zl, x, zh, 4, 2), DP + TP)
    return jax.shard_map(
        body,
        mesh=fine,
        in_specs=(
            P(DP + TP, None),
            P(DP, TP),
            P(DP, TP),
            P(TP, DP),
            P(TP, DP),
            P(TP, DP),
            P(TP),
        ),
        out_specs=(
            P(DP, TP),
            P(DP, TP),
            P(TP, DP),
            P(TP, DP),
            P(TP, DP),
        ),
        check_vma=False,
    )
```
